256 devices in a mesh: rep: 2 (over y_lo), blk: 128 (over x, y_hi, z, core).
Axes of the slice: x: 4, y: 4 (y_hi: 2, y_lo: 2; y = y_hi * 2 + y_lo), z: 8, core: 2. Of those that a mesh axis runs over, the one named last changes fastest.
Arguments:
- a_blocks: float32 [128, 48, 256, 256], P('blk', 'rep'), may hold values from -0.375 to 0.375
- a_rows: int32 [128, 48], P('blk', 'rep'), may hold values from 0 to 255, as said below
- a_cols: int32 [128, 48], P('blk', 'rep'), may hold values from 0 to 255, as said below
- b_blocks: float32 [128, 6, 256, 256], P('blk'), may hold values from -6 to 6
- b_rows: int32 [128, 6], P('blk'), may hold values from 0 to 255, as said below
- b_cols: int32 [128, 6], P('blk'), may hold values from 0 to 255
- b_count: int32 [128], P('blk'), may hold values from 1 to 6, as said below
- c_rows: int32 [128, 16], P('blk'), may hold values from 0 to 255, as said below
- c_cols: int32 [128, 16], P('blk'), may hold values from 0 to 255
Outputs:
- iterate: float32 [128, 16, 256, 256], P('blk', 'rep')
The draws below stay inside these ranges and needn't reach their ends.
Inputs may be any that keep to these rules, and one draw needn't show every extreme that they name: `a_rows`: entry [d, g] lies in the block rows d * 2 to d * 2 + 1. `a_cols`: entry [d, r * 6 * 4 + k * 4 + m] (m < 4) lies in the block rows e * 2 to e * 2 + 1 with e = (d + (r - 1) * 6 + k) modulo the size of blk. `b_rows`: entry [e, q] lies in the block rows e * 2 to e * 2 + 1. `b_count`: equals 6 on at least one index. `c_rows`: entry [d, t] lies in the block rows d * 2 to d * 2 + 1.
All inputs are finite; a program needn't handle non-finite values.
Results may differ from the reference program's by a relative error of at most 0.0003.
Values sent between devices are 32-bit elements; how exact they have to be, the bound alone decides.
No kernel may reach another device: no remote copies, remote signals or barrier semaphores. Data moves between devices by JAX's collectives and lax.ppermute only.
A program may use at most 128 MiB of HBM per device.

```python
import jax
import jax.numpy as jnp
from jax import lax

BLOCK = 256
RB_DEV = 2
STEPS = 6
PANEL = 6
A_SLOTS = 4
TARGETS = 16
N_REP = 2
N_BLK = 128


def pattern(key):
    subkeys = jax.random.split(jax.random.fold_in(key, 7171), 11)
    devices = jnp.arange(N_BLK, dtype=jnp.int32)[:, None]
    groups = jnp.arange(N_REP * STEPS * A_SLOTS, dtype=jnp.int32)[None, :] // A_SLOTS
    offset = groups - N_REP // 2 * STEPS
    shape_a = (N_BLK, N_REP * STEPS * A_SLOTS)
    a_rows = devices * RB_DEV + jax.random.randint(subkeys[0], shape_a, 0, RB_DEV, dtype=jnp.int32)
    owners = (devices + offset) % N_BLK
    a_cols = owners * RB_DEV + jax.random.randint(subkeys[1], shape_a, 0, RB_DEV, dtype=jnp.int32)
    shape_b = (N_BLK, PANEL)
    b_rows = devices * RB_DEV + jax.random.randint(subkeys[2], shape_b, 0, RB_DEV, dtype=jnp.int32)
    column_owner = (devices + jax.random.randint(subkeys[3], shape_b, 0, 2, dtype=jnp.int32)) % N_BLK
    b_cols = column_owner * RB_DEV + jax.random.randint(subkeys[4], shape_b, 0, RB_DEV, dtype=jnp.int32)
    first_count = jax.random.randint(subkeys[5], (N_BLK,), 1, PANEL + 1, dtype=jnp.int32)
    second_count = jax.random.randint(subkeys[6], (N_BLK,), 1, PANEL + 1, dtype=jnp.int32)
    fullest = jax.random.randint(subkeys[7], (), 0, N_BLK, dtype=jnp.int32)
    b_count = jnp.where(devices[:, 0] == fullest, PANEL, jnp.minimum(first_count, second_count)).astype(jnp.int32)
    shape_c = (N_BLK, TARGETS)
    reach = jax.random.randint(subkeys[8], shape_c, -(N_REP // 2) * STEPS, (N_REP - N_REP // 2) * STEPS + 1, dtype=jnp.int32)
    c_rows = devices * RB_DEV + jax.random.randint(subkeys[9], shape_c, 0, RB_DEV, dtype=jnp.int32)
    c_cols = (devices + reach) % N_BLK * RB_DEV + jax.random.randint(subkeys[10], shape_c, 0, RB_DEV, dtype=jnp.int32)
    return (a_rows, a_cols, b_rows, b_cols, b_count, c_rows, c_cols)


def draw_a_rows(key, part):
    return pattern(key)[0]


def draw_a_cols(key, part):
    return pattern(key)[1]


def draw_b_rows(key, part):
    return pattern(key)[2]


def draw_b_cols(key, part):
    return pattern(key)[3]


def draw_b_count(key, part):
    return pattern(key)[4]


def draw_c_rows(key, part):
    return pattern(key)[5]


def draw_c_cols(key, part):
    return pattern(key)[6]


def steps_of(rng, shape, pieces, least, top_value):
    level = 1.0
    for dim, parts in pieces:
        heights = jax.random.uniform(jax.random.fold_in(jax.random.fold_in(rng, 6), dim), (parts,), jnp.float32, least / len(pieces), top_value / len(pieces))
        level = level * jnp.repeat(jnp.exp(heights), shape[dim] // parts).reshape((-1,) + (1,) * (len(shape) - 1 - dim))
    return level


def scatter_about(key, shape, spread, bound, shards=(), held_as=jnp.bfloat16):
    drawn = spread * jax.random.normal(key, shape, jnp.float32)
    if shards:
        drawn = drawn * steps_of(key, shape, shards, -0.22, 0.18)
    return jnp.clip(drawn, -bound, bound).astype(held_as)


def setup_inputs(seed: int = 0) -> dict:
    splits = jax.random.split(jax.random.key(seed), 10)
    a_blocks = scatter_about(splits[0], (N_BLK, N_REP * STEPS * A_SLOTS, BLOCK, BLOCK), BLOCK ** -0.5, 0.375, ((0, 128), (1, 2)), jnp.float32)
    a_rows = draw_a_rows(jax.random.fold_in(splits[9], 71), 0)
    a_cols = draw_a_cols(jax.random.fold_in(splits[9], 71), 0)
    b_blocks = scatter_about(splits[3], (N_BLK, PANEL, BLOCK, BLOCK), 1.0, 6.0, ((0, 128),), jnp.float32)
    b_rows = draw_b_rows(jax.random.fold_in(splits[9], 71), 0)
    b_cols = draw_b_cols(jax.random.fold_in(splits[9], 71), 0)
    b_count = draw_b_count(jax.random.fold_in(splits[9], 71), 0)
    c_rows = draw_c_rows(jax.random.fold_in(splits[9], 71), 0)
    c_cols = draw_c_cols(jax.random.fold_in(splits[9], 71), 0)
    return dict(a_blocks=a_blocks, a_rows=a_rows, a_cols=a_cols, b_blocks=b_blocks, b_rows=b_rows, b_cols=b_cols, b_count=b_count, c_rows=c_rows, c_cols=c_cols)


def one_device(items, b_blocks, b_rows, b_cols, b_count):
    a_group, a_row, a_col, target_rows, target_cols = items
    owners = (a_col // RB_DEV).astype(jnp.int32)
    panels = jnp.take(b_blocks, owners, axis=0)
    panel_rows = jnp.take(b_rows, owners, axis=0)
    panel_cols = jnp.take(b_cols, owners, axis=0)
    counts = jnp.take(b_count, owners, axis=0)
    products = jnp.einsum("kij,kqjl->kqil", a_group, panels, precision=lax.Precision.HIGHEST)
    slot_index = jnp.arange(PANEL, dtype=jnp.int32)
    live = slot_index[None, :] < counts[:, None]
    weights = (a_row[None, :, None] == target_rows[:, None, None]) & (a_col[None, :, None] == panel_rows[None, :, :]) & (panel_cols[None, :, :] == target_cols[:, None, None]) & live[None, :, :]
    product = jnp.einsum("tkq,kqil->til", weights.astype(jnp.float32), products, precision=lax.Precision.HIGHEST)
    diagonal = (target_rows == target_cols).astype(jnp.float32)
    identity = jnp.eye(BLOCK, dtype=jnp.float32)
    return 1.5 * diagonal[:, None, None] * identity[None, :, :] - 0.5 * product


def reference(a_blocks, a_rows, a_cols, b_blocks, b_rows, b_cols, b_count, c_rows, c_cols):
    def apply(items):
        return one_device(items, b_blocks, b_rows, b_cols, b_count)

    return lax.map(apply, (a_blocks, a_rows, a_cols, c_rows, c_cols))
```

```python
import jax
import jax.numpy as jnp
from jax import lax
from jax.experimental import pallas as pl
from jax.experimental.pallas import tpu as pltpu
from jax.sharding import PartitionSpec as P


STEPS = 6
A_SLOTS = 4
PANEL = 6
HALF = 3
FRONT = 2
RUN = 8
REACH = 3
BOTH = ("rep", "blk")


def routed(value, target):
    n_rep, n_blk = lax.axis_size("rep"), lax.axis_size("blk")
    route = []
    for r in range(n_rep):
        for b in range(n_blk):
            r2, b2 = target(r, b)
            route.append((r * n_blk + b, r2 * n_blk + b2 % n_blk))
    return lax.ppermute(value, BOTH, route)


def upward(value):
    return routed(value, lambda r, b: (1 - r if (b // 2) % RUN == RUN - 1 else r, b + 2))


def downward(value):
    return routed(value, lambda r, b: (1 - r if (b // 2) % RUN == 0 else r, b - 2))


def other_replica(value):
    return routed(value, lambda r, b: (1 - r, b))


def other_core(value):
    return routed(value, lambda r, b: (r, b ^ 1))


def split(x):
    high = x.astype(jnp.bfloat16)
    low = (x - high.astype(jnp.float32)).astype(jnp.bfloat16)
    return high, low


def product(a, b):
    a_high, a_low = split(a)
    b_high, b_low = split(b)

    def dot(x, y):
        return jnp.dot(x, y, preferred_element_type=jnp.float32)

    return dot(a_high, b_high) + (dot(a_high, b_low) + dot(a_low, b_high))


def multiply_kernel(
    n_whole, n_split, first, last, info, a_rows, a_cols, c_rows, c_cols, *refs
):
    n_panels = n_whole + n_split
    notes, a_hbm, refs = refs[:n_panels], refs[n_panels], refs[n_panels + 1 :]
    whole, refs = refs[:n_whole], refs[n_whole:]
    pieces, refs = refs[: 4 * n_split], refs[4 * n_split :]
    if not first:
        acc_in, refs = refs[0], refs[1:]
    if last:
        keep_out, send_out, refs = refs[0], refs[1], refs[2:]
    else:
        acc_out, refs = refs[0], refs[1:]
    acc, a_buf, b_buf, work, hits, count, sems, acc_sem = refs
    size = a_buf.shape[-1]
    n_targets = acc.shape[0]
    half = n_targets // 2

    if not first:
        load = pltpu.make_async_copy(acc_in, acc, acc_sem.at[0])
        load.start()

    per_panel = A_SLOTS * PANEL
    count[0] = 0

    for p in range(n_panels):
        group = info[p]

        @pl.when(group >= 0)
        def _():
            @pl.loop(0, notes[p][2 * PANEL])
            def _(q):
                @pl.loop(0, A_SLOTS)
                def _(m):
                    slot = group * A_SLOTS + m

                    @pl.when(a_cols[slot] == notes[p][q])
                    def _():
                        row, col = a_rows[slot], notes[p][PANEL + q]
                        mask = jnp.int32(0)
                        for t in range(n_targets):
                            hit = (c_rows[t] == row) & (c_cols[t] == col)
                            mask = mask + jnp.where(hit, 1 << t, 0)

                        @pl.when(mask != 0)
                        def _():
                            n = count[0]
                            work[n] = p * per_panel + m * PANEL + q
                            hits[n] = mask
                            count[0] = n + 1

    total = count[0]

    def fetch_b(source, buf):
        pltpu.make_async_copy(source, b_buf.at[buf], sems.at[1, buf]).start()

    def fetch(n, buf):
        i = work[n]
        panel = lax.div(i, per_panel)
        rest = lax.rem(i, per_panel)
        a_slot = info[panel] * A_SLOTS + lax.div(rest, PANEL)
        q = lax.rem(rest, PANEL)
        pltpu.make_async_copy(a_hbm.at[a_slot], a_buf.at[buf], sems.at[0, buf]).start()
        for p in range(n_whole):

            @pl.when(panel == p)
            def _():
                fetch_b(whole[p].at[q], buf)

        second = (lax.rem(q, 2) != info[n_panels + panel]).astype(jnp.int32)
        place = lax.div(q, 2)
        tail = (place == FRONT).astype(jnp.int32)
        which = (panel - n_whole) * 4 + tail * 2 + second
        row = pl.multiple_of((place - tail * FRONT) * size, size)
        for p in range(4 * n_split):

            @pl.when(which == p)
            def _():
                if p % 4 < 2:
                    fetch_b(pieces[p].at[pl.ds(row, size), :], buf)
                else:
                    fetch_b(pieces[p].at[pl.ds((p % 4 - 2) * size if pieces[p].shape[0] > size else 0, size), :], buf)

    @pl.when(total > 0)
    def _():
        fetch(0, 0)

    if first:
        acc[...] = jnp.zeros_like(acc)
    else:
        load.wait()

    @pl.loop(0, total)
    def _(n):
        buf = lax.rem(n, 2)

        @pl.when(n + 1 < total)
        def _():
            fetch(n + 1, 1 - buf)

        pltpu.make_async_copy(a_hbm.at[0], a_buf.at[buf], sems.at[0, buf]).wait()
        pltpu.make_async_copy(a_hbm.at[0], b_buf.at[buf], sems.at[1, buf]).wait()
        term = product(a_buf[buf], b_buf[buf])
        mask = hits[n]

        @pl.loop(0, n_targets)
        def _(t):
            @pl.when(lax.rem(lax.shift_right_logical(mask, t), 2) == 1)
            def _():
                acc[t] = acc[t] + term

    if last:
        out = pltpu.make_async_copy(acc.at[pl.ds(half, half)], send_out, acc_sem.at[0])
        out.start()
        kept = pltpu.make_async_copy(acc.at[pl.ds(0, half)], keep_out, acc_sem.at[1])
        kept.start()
        out.wait()
        kept.wait()
    else:
        out = pltpu.make_async_copy(acc, acc_out, acc_sem.at[0])
        out.start()
        out.wait()


def multiply(info, tables, notes, a_blocks, whole, pieces, acc, last, n_targets):
    n_whole, n_split = len(whole), len(pieces) // 4
    n_panels = n_whole + n_split
    size = a_blocks.shape[-1]
    first = acc is None
    smem = pl.BlockSpec(memory_space=pltpu.SMEM)
    anywhere = pl.BlockSpec(memory_space=pl.ANY)
    stays = pl.BlockSpec(memory_space=pltpu.HBM)
    full = jax.ShapeDtypeStruct((n_targets, size, size), jnp.float32)
    part = jax.ShapeDtypeStruct((n_targets // 2, size, size), jnp.float32)
    numbers = [info, *tables, *notes]
    operands = [*numbers, a_blocks, *whole, *pieces] + ([] if first else [acc])

    def kernel(*refs):
        multiply_kernel(n_whole, n_split, first, last, *refs)

    return pl.pallas_call(
        kernel,
        out_shape=[part, part] if last else full,
        in_specs=[smem] * len(numbers) + [stays] + [anywhere] * (len(operands) - len(numbers) - 1),
        out_specs=[anywhere, anywhere] if last else anywhere,
        scratch_shapes=[
            pltpu.VMEM((n_targets, size, size), jnp.float32),
            pltpu.VMEM((2, size, size), jnp.float32),
            pltpu.VMEM((2, size, size), jnp.float32),
            pltpu.SMEM((n_panels * A_SLOTS * PANEL,), jnp.int32),
            pltpu.SMEM((n_panels * A_SLOTS * PANEL,), jnp.int32),
            pltpu.SMEM((1,), jnp.int32),
            pltpu.SemaphoreType.DMA((2, 2)),
            pltpu.SemaphoreType.DMA((2,)),
        ],
        cost_estimate=pl.CostEstimate(
            flops=2 * 8 * size**3, bytes_accessed=12 * 2**20, transcendentals=0
        ),
        compiler_params=pltpu.CompilerParams(vmem_limit_bytes=8 * 2**20),
        name="multiply",
    )(*operands)


def local(a_blocks, a_rows, a_cols, b_blocks, b_rows, b_cols, b_count, c_rows, c_cols):
    replica = lax.axis_index("rep")
    index = lax.axis_index("blk")
    core = index % 2
    z = (index // 2) % RUN
    lower = replica == 0
    a_blocks = a_blocks[0]
    b_blocks = b_blocks[0]
    size = a_blocks.shape[-1]
    n_targets = c_rows.shape[1]
    half = n_targets // 2

    numbers = jnp.concatenate([b_rows[0], b_cols[0], b_count, jnp.zeros((3,), jnp.int32)])
    notes = jnp.pad(numbers.astype(jnp.float32)[None], ((0, 7), (0, size - numbers.shape[0])))
    mine = lax.dynamic_index_in_dim(
        b_blocks.reshape(HALF, 2, size, size), replica, 1, keepdims=False
    )
    front = jnp.concatenate([mine[:FRONT].reshape(FRONT * size, size), notes], 0)
    up = down = front
    up_tail = down_tail = mine[FRONT]

    def own_first(x):
        return jnp.where(lower, x, jnp.roll(x, half))

    target_rows = own_first(c_rows[0])
    target_cols = own_first(c_cols[0])
    tables = [a_rows[0], a_cols[0], target_rows, target_cols]

    def group_of(distance):
        group = distance + jnp.where(lower, STEPS, 0)
        return jnp.where((group >= 0) & (group < STEPS), group, -1)

    def noted(piece):
        return piece[FRONT * size, : numbers.shape[0]].astype(jnp.int32)

    side = jnp.where(lower, -1, 1)
    zero = jnp.int32(0)

    def run(stages, whole, acc, last):
        pieces, notes, groups, lows = [], [], [], []
        for p, m, g, l in stages:
            pieces += p
            notes += m
            groups += g
            lows += l
        info = jnp.stack(groups + lows).astype(jnp.int32)
        return multiply(info, tables, notes, a_blocks, whole, pieces, acc, last, n_targets)

    ups, downs, up_tails, down_tails = [], [], [], []
    for _ in range(1, REACH + 1):
        up, down = upward(up), downward(down)
        up_tail, down_tail = upward(up_tail), downward(down_tail)
        ups.append(up)
        downs.append(down)
        up_tails.append(up_tail)
        down_tails.append(down_tail)
    partner = other_core(b_blocks)
    notes = [numbers, other_core(numbers)]
    stages = [([], notes, [group_of(zero), group_of(1 - 2 * core)], [zero, zero])]
    for s in range(1, REACH + 1):
        up, down, up_tail, down_tail = ups[s - 1], downs[s - 1], up_tails[s - 1], down_tails[s - 1]
        kept, given = jnp.where(lower, up, down), jnp.where(lower, down, up)
        rest = other_replica(given)
        kept_tail = jnp.where(lower, up_tail, down_tail)
        rest_tail = other_replica(jnp.where(lower, down_tail, up_tail))
        kept2, rest2 = other_core(kept), other_core(rest)
        tails = jnp.concatenate([kept_tail, rest_tail], 0)
        tails2 = other_core(tails)
        crossed = jnp.where(lower, z < s, z + s > RUN - 1).astype(jnp.int32)
        low = lax.bitwise_xor(replica, crossed)
        notes = [noted(kept), noted(kept2)]
        groups = [group_of(2 * s * side), group_of(2 * s * side + 1 - 2 * core)]
        pieces = [kept, rest, tails, tails, kept2, rest2, tails2, tails2]
        stages.append((pieces, notes, groups, [low, low]))
    acc = run(stages[:REACH], [b_blocks, partner], None, False)
    keep, send = run(stages[REACH:], [], acc, True)
    summed = keep + other_replica(send)
    diagonal = (target_rows[:half] == target_cols[:half]).astype(jnp.float32)
    identity = jnp.eye(size, dtype=jnp.float32)
    result = 1.5 * diagonal[:, None, None] * identity[None, :, :] - 0.5 * summed
    return result[None]


def solution(mesh):
    return jax.shard_map(
        local,
        mesh=mesh,
        in_specs=(
            P("blk", "rep", None, None),
            P("blk", "rep"),
            P("blk", "rep"),
            P("blk", None, None, None),
            P("blk", None),
            P("blk", None),
            P("blk"),
            P("blk", None),
            P("blk", None),
        ),
        out_specs=P("blk", "rep", None, None),
        check_vma=False,
    )
```

```python
import functools

import jax
import jax.numpy as jnp
from jax import lax
from jax.experimental import pallas as pl
from jax.experimental.pallas import tpu as pltpu
from jax.sharding import PartitionSpec as P


STEPS = 6
A_SLOTS = 4
PANEL = 6
HALF = 3
FRONT = 2
RUN = 8
REACH = 3
BOTH = ("rep", "blk")


def routed(value, target):
    n_rep, n_blk = lax.axis_size("rep"), lax.axis_size("blk")
    route = []
    for r in range(n_rep):
        for b in range(n_blk):
            r2, b2 = target(r, b)
            route.append((r * n_blk + b, r2 * n_blk + b2 % n_blk))
    return lax.ppermute(value, BOTH, route)


def upward(value):
    return routed(value, lambda r, b: (1 - r if (b // 2) % RUN == RUN - 1 else r, b + 2))


def downward(value):
    return routed(value, lambda r, b: (1 - r if (b // 2) % RUN == 0 else r, b - 2))


def other_replica(value):
    return routed(value, lambda r, b: (1 - r, b))


def other_core(value):
    return routed(value, lambda r, b: (r, b ^ 1))


def split(x):
    high = x.astype(jnp.bfloat16)
    low = (x - high.astype(jnp.float32)).astype(jnp.bfloat16)
    return high, low


def product(a, b):
    a_high, a_low = split(a)
    b_high, b_low = split(b)

    def dot(x, y):
        return jnp.dot(x, y, preferred_element_type=jnp.float32)

    return dot(a_high, b_high) + (dot(a_high, b_low) + dot(a_low, b_high))


def scan_kernel(n_early, info, a_rows, a_cols, c_rows, c_cols, *refs):
    notes, (told, *lists) = refs[:-5], refs[-5:]
    for i in range(told.shape[0]):
        told[i] = 0
    for p in range(len(notes)):
        group = info[p]
        late = int(p >= n_early)
        work, hits = lists[2 * late], lists[2 * late + 1]

        @pl.when(group >= 0)
        def _():
            @pl.loop(0, notes[p][2 * PANEL])
            def _(q):
                @pl.loop(0, A_SLOTS)
                def _(m):
                    slot = group * A_SLOTS + m

                    @pl.when(a_cols[slot] == notes[p][q])
                    def _():
                        row, col = a_rows[slot], notes[p][PANEL + q]
                        mask = jnp.int32(0)
                        for t in range(c_rows.shape[0]):
                            hit = (c_rows[t] == row) & (c_cols[t] == col)
                            mask = mask + jnp.where(hit, 1 << t, 0)

                        @pl.when(mask != 0)
                        def _():
                            n = told[1 + late]
                            work[n] = ((p - late * n_early) * A_SLOTS + m) * PANEL + q
                            hits[n] = mask
                            told[1 + late] = n + 1
                            told[0] = told[0] | mask


def scan(info, tables, notes, n_early):
    smem = pl.BlockSpec(memory_space=pltpu.SMEM)
    sizes = [8] + 2 * [n_early * A_SLOTS * PANEL] + 2 * [(len(notes) - n_early) * A_SLOTS * PANEL]
    return pl.pallas_call(
        functools.partial(scan_kernel, n_early),
        out_shape=[jax.ShapeDtypeStruct((n,), jnp.int32) for n in sizes],
        in_specs=[smem] * (5 + len(notes)),
        out_specs=[smem] * 5,
        compiler_params=pltpu.CompilerParams(vmem_limit_bytes=2**20),
        name="scan",
    )(info, *tables, *notes)


def multiply_kernel(n_whole, n_split, last, info, told, work, hits, *refs):
    n_known = info.shape[0] // 2
    base = n_known - n_split if last else 0
    if last:
        theirs, c_rows, c_cols, refs = *refs[:3], refs[3:]
    a_hbm, refs = refs[0], refs[1:]
    whole, refs = refs[:n_whole], refs[n_whole:]
    pieces, refs = refs[: 4 * n_split], refs[4 * n_split :]
    if last:
        acc_in, keep_out, send_out, plan, refs = *refs[:4], refs[4:]
    else:
        acc_out, refs = refs[0], refs[1:]
    acc, a_buf, b_buf, sems, acc_sem = refs
    size = a_buf.shape[-1]
    n_targets = acc.shape[0]
    half = n_targets // 2

    if last:
        load = pltpu.make_async_copy(acc_in, acc, acc_sem.at[0])
        load.start()

    per_panel = A_SLOTS * PANEL
    total = told[1 + int(last)]

    def fetch_b(source, buf):
        pltpu.make_async_copy(source, b_buf.at[buf], sems.at[1, buf]).start()

    def fetch(n, buf):
        i = work[n]
        panel = lax.div(i, per_panel)
        rest = lax.rem(i, per_panel)
        a_slot = info[base + panel] * A_SLOTS + lax.div(rest, PANEL)
        q = lax.rem(rest, PANEL)
        pltpu.make_async_copy(a_hbm.at[a_slot], a_buf.at[buf], sems.at[0, buf]).start()
        for p in range(n_whole):

            @pl.when(panel == p)
            def _():
                fetch_b(whole[p].at[q], buf)

        second = (lax.rem(q, 2) != info[n_known + base + panel]).astype(jnp.int32)
        place = lax.div(q, 2)
        tail = (place == FRONT).astype(jnp.int32)
        which = (panel - n_whole) * 4 + tail * 2 + second
        row = pl.multiple_of((place - tail * FRONT) * size, size)
        for p in range(4 * n_split):

            @pl.when(which == p)
            def _():
                if p % 4 < 2:
                    fetch_b(pieces[p].at[pl.ds(row, size), :], buf)
                else:
                    fetch_b(pieces[p].at[pl.ds((p % 4 - 2) * size if pieces[p].shape[0] > size else 0, size), :], buf)

    @pl.when(total > 0)
    def _():
        fetch(0, 0)

    if last:
        load.wait()
    else:
        acc[...] = jnp.zeros_like(acc)

    @pl.loop(0, total)
    def _(n):
        buf = lax.rem(n, 2)

        @pl.when(n + 1 < total)
        def _():
            fetch(n + 1, 1 - buf)

        pltpu.make_async_copy(a_hbm.at[0], a_buf.at[buf], sems.at[0, buf]).wait()
        pltpu.make_async_copy(a_hbm.at[0], b_buf.at[buf], sems.at[1, buf]).wait()
        term = product(a_buf[buf], b_buf[buf])
        mask = hits[n]

        @pl.loop(0, n_targets)
        def _(t):
            @pl.when(lax.rem(lax.shift_right_logical(mask, t), 2) == 1)
            def _():
                acc[t] = acc[t] + term

    if last:
        kept = pltpu.make_async_copy(acc.at[pl.ds(0, half)], keep_out, acc_sem.at[1])
        kept.start()
        sent, come = jnp.int32(0), jnp.int32(0)
        for t in range(half):
            goes = lax.rem(lax.shift_right_logical(told[0], half + t), 2)
            comes = lax.rem(lax.shift_right_logical(theirs[0], half + t), 2)

            @pl.when(goes == 1)
            def _():
                pltpu.make_async_copy(acc.at[half + t], send_out.at[sent], acc_sem.at[0]).start()

            plan[8 + t] = come
            plan[16 + t] = comes
            plan[24 + t] = (c_rows[t] == c_cols[t]).astype(jnp.int32)
            sent, come = sent + goes, come + comes
        plan[0] = jnp.maximum(jnp.maximum(sent, come), 1) - 1
        for t in range(1, 8):
            plan[t] = 0

        @pl.loop(0, sent)
        def _(n):
            pltpu.make_async_copy(acc.at[half], send_out.at[n], acc_sem.at[0]).wait()

        kept.wait()
    else:
        out = pltpu.make_async_copy(acc, acc_out, acc_sem.at[0])
        out.start()
        out.wait()


def multiply(info, found, theirs, a_blocks, whole, pieces, acc, n_targets):
    n_whole, n_split = len(whole), len(pieces) // 4
    size = a_blocks.shape[-1]
    last = acc is not None
    smem = pl.BlockSpec(memory_space=pltpu.SMEM)
    anywhere = pl.BlockSpec(memory_space=pl.ANY)
    full = jax.ShapeDtypeStruct((n_targets, size, size), jnp.float32)
    part = jax.ShapeDtypeStruct((n_targets // 2, size, size), jnp.float32)
    plan = jax.ShapeDtypeStruct((32,), jnp.int32)
    numbers = [info, *found, *theirs]
    blocks = [a_blocks, *whole, *pieces] + ([acc] if last else [])

    def kernel(*refs):
        multiply_kernel(n_whole, n_split, last, *refs)

    return pl.pallas_call(
        kernel,
        out_shape=[part, part, plan] if last else full,
        in_specs=[smem] * len(numbers) + [anywhere] * len(blocks),
        out_specs=[anywhere, anywhere, smem] if last else anywhere,
        scratch_shapes=[
            pltpu.VMEM((n_targets, size, size), jnp.float32),
            pltpu.VMEM((2, size, size), jnp.float32),
            pltpu.VMEM((2, size, size), jnp.float32),
            pltpu.SemaphoreType.DMA((2, 2)),
            pltpu.SemaphoreType.DMA((2,)),
        ],
        cost_estimate=pl.CostEstimate(
            flops=2 * 8 * size**3, bytes_accessed=12 * 2**20, transcendentals=0
        ),
        compiler_params=pltpu.CompilerParams(vmem_limit_bytes=8 * 2**20),
        name="multiply",
    )(*numbers, *blocks)


def local(a_blocks, a_rows, a_cols, b_blocks, b_rows, b_cols, b_count, c_rows, c_cols):
    replica = lax.axis_index("rep")
    index = lax.axis_index("blk")
    core = index % 2
    z = (index // 2) % RUN
    lower = replica == 0
    a_blocks = a_blocks[0]
    b_blocks = b_blocks[0]
    size = a_blocks.shape[-1]
    n_targets = c_rows.shape[1]
    half = n_targets // 2

    numbers = jnp.concatenate([b_rows[0], b_cols[0], b_count, jnp.zeros((3,), jnp.int32)])
    notes = jnp.pad(numbers.astype(jnp.float32)[None], ((0, 7), (0, size - numbers.shape[0])))
    mine = lax.dynamic_index_in_dim(
        b_blocks.reshape(HALF, 2, size, size), replica, 1, keepdims=False
    )
    front = jnp.concatenate([mine[:FRONT].reshape(FRONT * size, size), notes], 0)
    up = down = front
    up_tail = down_tail = mine[FRONT]

    def own_first(x):
        return jnp.where(lower, x, jnp.roll(x, half))

    target_rows = own_first(c_rows[0])
    target_cols = own_first(c_cols[0])
    tables = [a_rows[0], a_cols[0], target_rows, target_cols]

    def group_of(distance):
        group = distance + jnp.where(lower, STEPS, 0)
        return jnp.where((group >= 0) & (group < STEPS), group, -1)

    def noted(piece):
        return piece[FRONT * size, : numbers.shape[0]].astype(jnp.int32)

    side = jnp.where(lower, -1, 1)
    zero = jnp.int32(0)

    ups, downs, up_tails, down_tails = [], [], [], []
    for _ in range(1, REACH + 1):
        up, down = upward(up), downward(down)
        up_tail, down_tail = upward(up_tail), downward(down_tail)
        ups.append(up)
        downs.append(down)
        up_tails.append(up_tail)
        down_tails.append(down_tail)
    partner = other_core(b_blocks)
    notes = [numbers, other_core(numbers)]
    stages = [([], notes, [group_of(zero), group_of(1 - 2 * core)], [zero, zero])]
    for s in range(1, REACH + 1):
        up, down, up_tail, down_tail = ups[s - 1], downs[s - 1], up_tails[s - 1], down_tails[s - 1]
        kept, given = jnp.where(lower, up, down), jnp.where(lower, down, up)
        rest = other_replica(given)
        kept_tail = jnp.where(lower, up_tail, down_tail)
        rest_tail = other_replica(jnp.where(lower, down_tail, up_tail))
        kept2, rest2 = other_core(kept), other_core(rest)
        tails = jnp.concatenate([kept_tail, rest_tail], 0)
        tails2 = other_core(tails)
        crossed = jnp.where(lower, z < s, z + s > RUN - 1).astype(jnp.int32)
        low = lax.bitwise_xor(replica, crossed)
        notes = [noted(kept), noted(kept2)]
        groups = [group_of(2 * s * side), group_of(2 * s * side + 1 - 2 * core)]
        pieces = [kept, rest, tails, tails, kept2, rest2, tails2, tails2]
        stages.append((pieces, notes, groups, [low, low]))

    def of(part, i):
        return [x for stage in part for x in stage[i]]

    early, late = stages[:REACH], stages[REACH:]
    info = jnp.stack(of(stages, 2) + of(stages, 3))
    told, work0, hits0, work1, hits1 = scan(
        info, tables, of(stages, 1), len(of(early, 1))
    )
    theirs = other_replica(told)
    acc = multiply(
        info, [told, work0, hits0], [], a_blocks, [b_blocks, partner], of(early, 0), None, n_targets
    )
    keep, send, plan = multiply(
        info,
        [told, work1, hits1],
        [theirs, target_rows, target_cols],
        a_blocks,
        [],
        of(late, 0),
        acc,
        n_targets,
    )
    result = lax.switch(
        plan[0], [functools.partial(finish, n + 1) for n in range(half)], keep, send, plan
    )
    return result[None]


def finish_kernel(plan, keep, come, out):
    t = pl.program_id(0)
    size = out.shape[-1]
    row = lax.broadcasted_iota(jnp.int32, (size, size), 0)
    col = lax.broadcasted_iota(jnp.int32, (size, size), 1)
    unit = jnp.where((row == col) & (plan[24 + t] == 1), 1.5, 0.0)

    @pl.when(plan[16 + t] == 1)
    def _():
        out[...] = unit - 0.5 * (keep[...] + come[...])

    @pl.when(plan[16 + t] == 0)
    def _():
        out[...] = unit - 0.5 * keep[...]


def finish(many, keep, send, plan):
    half, size = keep.shape[0], keep.shape[-1]
    come = other_replica(send[:many])
    block = (None, size, size)
    return pl.pallas_call(
        finish_kernel,
        out_shape=jax.ShapeDtypeStruct(keep.shape, jnp.float32),
        grid_spec=pltpu.PrefetchScalarGridSpec(
            num_scalar_prefetch=1,
            grid=(half,),
            in_specs=[
                pl.BlockSpec(block, lambda t, plan: (t, 0, 0)),
                pl.BlockSpec(block, lambda t, plan: (jnp.minimum(plan[8 + t], many - 1), 0, 0)),
            ],
            out_specs=pl.BlockSpec(block, lambda t, plan: (t, 0, 0)),
        ),
        compiler_params=pltpu.CompilerParams(
            dimension_semantics=("arbitrary",), vmem_limit_bytes=4 * 2**20
        ),
        name="finish",
    )(plan, keep, come)


def solution(mesh):
    return jax.shard_map(
        local,
        mesh=mesh,
        in_specs=(
            P("blk", "rep", None, None),
            P("blk", "rep"),
            P("blk", "rep"),
            P("blk", None, None, None),
            P("blk", None),
            P("blk", None),
            P("blk"),
            P("blk", None),
            P("blk", None),
        ),
        out_specs=P("blk", "rep", None, None),
        check_vma=False,
    )
```

```python
import functools

import jax
import jax.numpy as jnp
from jax import lax
from jax.experimental import pallas as pl
from jax.experimental.pallas import tpu as pltpu
from jax.sharding import PartitionSpec as P


STEPS = 6
A_SLOTS = 4
PANEL = 6
HALF = 3
FRONT = 2
RUN = 8
REACH = 3
BOTH = ("rep", "blk")


def routed(value, target):
    n_rep, n_blk = lax.axis_size("rep"), lax.axis_size("blk")
    route = []
    for r in range(n_rep):
        for b in range(n_blk):
            r2, b2 = target(r, b)
            route.append((r * n_blk + b, r2 * n_blk + b2 % n_blk))
    return lax.ppermute(value, BOTH, route)


def upward(value):
    return routed(value, lambda r, b: (1 - r if (b // 2) % RUN == RUN - 1 else r, b + 2))


def downward(value):
    return routed(value, lambda r, b: (1 - r if (b // 2) % RUN == 0 else r, b - 2))


def other_replica(value):
    return routed(value, lambda r, b: (1 - r, b))


def other_core(value):
    return routed(value, lambda r, b: (r, b ^ 1))


def split(x):
    high = x.astype(jnp.bfloat16)
    low = (x - high.astype(jnp.float32)).astype(jnp.bfloat16)
    return high, low


def product(a, b):
    a_high, a_low = split(a)
    b_high, b_low = split(b)

    def dot(x, y):
        return jnp.dot(x, y, preferred_element_type=jnp.float32)

    return dot(a_high, b_high) + (dot(a_high, b_low) + dot(a_low, b_high))


def scan_kernel(counts, first, before, info, a_rows, a_cols, c_rows, c_cols, *refs):
    n_out = 1 + 2 * len(counts)
    notes, (told, *lists) = refs[:-n_out], refs[-n_out:]
    told[0] = before[0]
    for i in range(1, told.shape[0]):
        told[i] = 0
    places = [(part, i) for part, n in enumerate(counts) for i in range(n)]
    for p, (part, inside) in enumerate(places):
        group = info[first + p]
        work, hits = lists[2 * part], lists[2 * part + 1]

        @pl.when(group >= 0)
        def _():
            @pl.loop(0, notes[p][2 * PANEL])
            def _(q):
                @pl.loop(0, A_SLOTS)
                def _(m):
                    slot = group * A_SLOTS + m

                    @pl.when(a_cols[slot] == notes[p][q])
                    def _():
                        row, col = a_rows[slot], notes[p][PANEL + q]
                        mask = jnp.int32(0)
                        for t in range(c_rows.shape[0]):
                            hit = (c_rows[t] == row) & (c_cols[t] == col)
                            mask = mask + jnp.where(hit, 1 << t, 0)

                        @pl.when(mask != 0)
                        def _():
                            n = told[1 + part]
                            work[n] = (inside * A_SLOTS + m) * PANEL + q
                            hits[n] = mask
                            told[1 + part] = n + 1
                            told[0] = told[0] | mask


def scan(counts, first, before, info, tables, notes):
    smem = pl.BlockSpec(memory_space=pltpu.SMEM)
    sizes = [8] + [n * A_SLOTS * PANEL for n in counts for _ in range(2)]
    return pl.pallas_call(
        functools.partial(scan_kernel, counts, first),
        out_shape=[jax.ShapeDtypeStruct((n,), jnp.int32) for n in sizes],
        in_specs=[smem] * (6 + len(notes)),
        out_specs=[smem] * len(sizes),
        compiler_params=pltpu.CompilerParams(vmem_limit_bytes=2**20),
        name="scan",
    )(before, info, *tables, *notes)


def multiply_kernel(n_whole, n_split, base, part, first, last, info, told, work, hits, *refs):
    n_known = info.shape[0] // 2
    if last:
        theirs, c_rows, c_cols, refs = *refs[:3], refs[3:]
    a_hbm, refs = refs[0], refs[1:]
    whole, refs = refs[:n_whole], refs[n_whole:]
    pieces, refs = refs[: 4 * n_split], refs[4 * n_split :]
    if not first:
        acc_in, refs = refs[0], refs[1:]
    if last:
        keep_out, send_out, plan, refs = *refs[:3], refs[3:]
    else:
        acc_out, refs = refs[0], refs[1:]
    acc, a_buf, b_buf, sems, acc_sem = refs
    size = a_buf.shape[-1]
    n_targets = acc.shape[0]
    half = n_targets // 2

    if not first:
        load = pltpu.make_async_copy(acc_in, acc, acc_sem.at[0])
        load.start()

    per_panel = A_SLOTS * PANEL
    total = told[1 + part]

    def fetch_b(source, buf):
        pltpu.make_async_copy(source, b_buf.at[buf], sems.at[1, buf]).start()

    def fetch(n, buf):
        i = work[n]
        panel = lax.div(i, per_panel)
        rest = lax.rem(i, per_panel)
        a_slot = info[base + panel] * A_SLOTS + lax.div(rest, PANEL)
        q = lax.rem(rest, PANEL)
        pltpu.make_async_copy(a_hbm.at[a_slot], a_buf.at[buf], sems.at[0, buf]).start()
        for p in range(n_whole):

            @pl.when(panel == p)
            def _():
                fetch_b(whole[p].at[q], buf)

        second = (lax.rem(q, 2) != info[n_known + base + panel]).astype(jnp.int32)
        place = lax.div(q, 2)
        tail = (place == FRONT).astype(jnp.int32)
        which = (panel - n_whole) * 4 + tail * 2 + second
        row = pl.multiple_of((place - tail * FRONT) * size, size)
        for p in range(4 * n_split):

            @pl.when(which == p)
            def _():
                if p % 4 < 2:
                    fetch_b(pieces[p].at[pl.ds(row, size), :], buf)
                else:
                    fetch_b(pieces[p].at[pl.ds((p % 4 - 2) * size if pieces[p].shape[0] > size else 0, size), :], buf)

    @pl.when(total > 0)
    def _():
        fetch(0, 0)

    if first:
        acc[...] = jnp.zeros_like(acc)
    else:
        load.wait()

    @pl.loop(0, total)
    def _(n):
        buf = lax.rem(n, 2)

        @pl.when(n + 1 < total)
        def _():
            fetch(n + 1, 1 - buf)

        pltpu.make_async_copy(a_hbm.at[0], a_buf.at[buf], sems.at[0, buf]).wait()
        pltpu.make_async_copy(a_hbm.at[0], b_buf.at[buf], sems.at[1, buf]).wait()
        term = product(a_buf[buf], b_buf[buf])
        mask = hits[n]

        @pl.loop(0, n_targets)
        def _(t):
            @pl.when(lax.rem(lax.shift_right_logical(mask, t), 2) == 1)
            def _():
                acc[t] = acc[t] + term

    if last:
        kept = pltpu.make_async_copy(acc.at[pl.ds(0, half)], keep_out, acc_sem.at[1])
        kept.start()
        sent, come = jnp.int32(0), jnp.int32(0)
        for t in range(half):
            goes = lax.rem(lax.shift_right_logical(told[0], half + t), 2)
            comes = lax.rem(lax.shift_right_logical(theirs[0], half + t), 2)

            @pl.when(goes == 1)
            def _():
                pltpu.make_async_copy(acc.at[half + t], send_out.at[sent], acc_sem.at[0]).start()

            plan[8 + t] = come
            plan[16 + t] = comes
            plan[24 + t] = (c_rows[t] == c_cols[t]).astype(jnp.int32)
            sent, come = sent + goes, come + comes
        plan[0] = jnp.maximum(jnp.maximum(sent, come), 1) - 1
        for t in range(1, 8):
            plan[t] = 0

        @pl.loop(0, sent)
        def _(n):
            pltpu.make_async_copy(acc.at[half], send_out.at[n], acc_sem.at[0]).wait()

        kept.wait()
    else:
        out = pltpu.make_async_copy(acc, acc_out, acc_sem.at[0])
        out.start()
        out.wait()


def multiply(info, found, base, part, theirs, a_blocks, whole, pieces, acc, n_targets):
    n_whole, n_split = len(whole), len(pieces) // 4
    size = a_blocks.shape[-1]
    first, last = acc is None, theirs != []
    smem = pl.BlockSpec(memory_space=pltpu.SMEM)
    anywhere = pl.BlockSpec(memory_space=pl.ANY)
    full = jax.ShapeDtypeStruct((n_targets, size, size), jnp.float32)
    share = jax.ShapeDtypeStruct((n_targets // 2, size, size), jnp.float32)
    plan = jax.ShapeDtypeStruct((32,), jnp.int32)
    numbers = [info, *found, *theirs]
    blocks = [a_blocks, *whole, *pieces] + ([] if first else [acc])

    def kernel(*refs):
        multiply_kernel(n_whole, n_split, base, part, first, last, *refs)

    return pl.pallas_call(
        kernel,
        out_shape=[share, share, plan] if last else full,
        in_specs=[smem] * len(numbers) + [anywhere] * len(blocks),
        out_specs=[anywhere, anywhere, smem] if last else anywhere,
        scratch_shapes=[
            pltpu.VMEM((n_targets, size, size), jnp.float32),
            pltpu.VMEM((2, size, size), jnp.float32),
            pltpu.VMEM((2, size, size), jnp.float32),
            pltpu.SemaphoreType.DMA((2, 2)),
            pltpu.SemaphoreType.DMA((2,)),
        ],
        cost_estimate=pl.CostEstimate(
            flops=2 * 8 * size**3, bytes_accessed=12 * 2**20, transcendentals=0
        ),
        compiler_params=pltpu.CompilerParams(vmem_limit_bytes=8 * 2**20),
        name="multiply",
    )(*numbers, *blocks)


def local(a_blocks, a_rows, a_cols, b_blocks, b_rows, b_cols, b_count, c_rows, c_cols):
    replica = lax.axis_index("rep")
    index = lax.axis_index("blk")
    core = index % 2
    z = (index // 2) % RUN
    lower = replica == 0
    a_blocks = a_blocks[0]
    b_blocks = b_blocks[0]
    size = a_blocks.shape[-1]
    n_targets = c_rows.shape[1]
    half = n_targets // 2

    numbers = jnp.concatenate([b_rows[0], b_cols[0], b_count, jnp.zeros((3,), jnp.int32)])
    notes = jnp.pad(numbers.astype(jnp.float32)[None], ((0, 7), (0, size - numbers.shape[0])))
    mine = lax.dynamic_index_in_dim(
        b_blocks.reshape(HALF, 2, size, size), replica, 1, keepdims=False
    )
    front = jnp.concatenate([mine[:FRONT].reshape(FRONT * size, size), notes], 0)
    up = down = front
    up_tail = down_tail = mine[FRONT]

    def own_first(x):
        return jnp.where(lower, x, jnp.roll(x, half))

    target_rows = own_first(c_rows[0])
    target_cols = own_first(c_cols[0])
    tables = [a_rows[0], a_cols[0], target_rows, target_cols]

    def group_of(distance):
        group = distance + jnp.where(lower, STEPS, 0)
        return jnp.where((group >= 0) & (group < STEPS), group, -1)

    def noted(piece):
        return piece[FRONT * size, : numbers.shape[0]].astype(jnp.int32)

    side = jnp.where(lower, -1, 1)
    zero = jnp.int32(0)

    ups, downs, up_tails, down_tails = [], [], [], []
    for _ in range(1, REACH + 1):
        up, down = upward(up), downward(down)
        up_tail, down_tail = upward(up_tail), downward(down_tail)
        ups.append(up)
        downs.append(down)
        up_tails.append(up_tail)
        down_tails.append(down_tail)
    partner = other_core(b_blocks)
    notes = [numbers, other_core(numbers)]
    stages = [([], notes, [group_of(zero), group_of(1 - 2 * core)], [zero, zero])]
    for s in range(1, REACH + 1):
        up, down, up_tail, down_tail = ups[s - 1], downs[s - 1], up_tails[s - 1], down_tails[s - 1]
        kept, given = jnp.where(lower, up, down), jnp.where(lower, down, up)
        rest = other_replica(given)
        kept_tail = jnp.where(lower, up_tail, down_tail)
        rest_tail = other_replica(jnp.where(lower, down_tail, up_tail))
        kept2, rest2 = other_core(kept), other_core(rest)
        tails = jnp.concatenate([kept_tail, rest_tail], 0)
        tails2 = other_core(tails)
        crossed = jnp.where(lower, z < s, z + s > RUN - 1).astype(jnp.int32)
        low = lax.bitwise_xor(replica, crossed)
        notes = [noted(kept), noted(kept2)]
        groups = [group_of(2 * s * side), group_of(2 * s * side + 1 - 2 * core)]
        pieces = [kept, rest, tails, tails, kept2, rest2, tails2, tails2]
        stages.append((pieces, notes, groups, [low, low]))

    def of(part, i):
        return [x for stage in part for x in stage[i]]

    info = jnp.stack(of(stages, 2) + of(stages, 3))
    near, middle, far = stages[:2], stages[2:3], stages[3:]
    found0 = scan([4], 0, jnp.zeros((8,), jnp.int32), info, tables, of(near, 1))
    acc = multiply(
        info, found0, 0, 0, [], a_blocks, [b_blocks, partner], of(near, 0), None, n_targets
    )
    told, work1, hits1, work2, hits2 = scan(
        [2, 2], 4, found0[0], info, tables, of(middle, 1) + of(far, 1)
    )
    theirs = other_replica(told)
    found1 = [told, work1, hits1]
    acc = multiply(info, found1, 4, 0, [], a_blocks, [], of(middle, 0), acc, n_targets)
    keep, send, plan = multiply(
        info,
        [told, work2, hits2],
        6,
        1,
        [theirs, target_rows, target_cols],
        a_blocks,
        [],
        of(far, 0),
        acc,
        n_targets,
    )
    result = lax.switch(
        plan[0], [functools.partial(finish, n + 1) for n in range(half)], keep, send, plan
    )
    return result[None]


def finish_kernel(plan, keep, come, out):
    t = pl.program_id(0)
    size = out.shape[-1]
    row = lax.broadcasted_iota(jnp.int32, (size, size), 0)
    col = lax.broadcasted_iota(jnp.int32, (size, size), 1)
    unit = jnp.where((row == col) & (plan[24 + t] == 1), 1.5, 0.0)

    @pl.when(plan[16 + t] == 1)
    def _():
        out[...] = unit - 0.5 * (keep[...] + come[...])

    @pl.when(plan[16 + t] == 0)
    def _():
        out[...] = unit - 0.5 * keep[...]


def finish(many, keep, send, plan):
    half, size = keep.shape[0], keep.shape[-1]
    come = other_replica(send[:many])
    block = (None, size, size)
    return pl.pallas_call(
        finish_kernel,
        out_shape=jax.ShapeDtypeStruct(keep.shape, jnp.float32),
        grid_spec=pltpu.PrefetchScalarGridSpec(
            num_scalar_prefetch=1,
            grid=(half,),
            in_specs=[
                pl.BlockSpec(block, lambda t, plan: (t, 0, 0)),
                pl.BlockSpec(block, lambda t, plan: (jnp.minimum(plan[8 + t], many - 1), 0, 0)),
            ],
            out_specs=pl.BlockSpec(block, lambda t, plan: (t, 0, 0)),
        ),
        compiler_params=pltpu.CompilerParams(
            dimension_semantics=("arbitrary",), vmem_limit_bytes=4 * 2**20
        ),
        name="finish",
    )(plan, keep, come)


def solution(mesh):
    return jax.shard_map(
        local,
        mesh=mesh,
        in_specs=(
            P("blk", "rep", None, None),
            P("blk", "rep"),
            P("blk", "rep"),
            P("blk", None, None, None),
            P("blk", None),
            P("blk", None),
            P("blk"),
            P("blk", None),
            P("blk", None),
        ),
        out_specs=P("blk", "rep", None, None),
        check_vma=False,
    )
```

```python
import functools

import jax
import jax.numpy as jnp
from jax import lax
from jax.experimental import pallas as pl
from jax.experimental.pallas import tpu as pltpu
from jax.sharding import PartitionSpec as P


STEPS = 6
A_SLOTS = 4
PANEL = 6
HALF = 3
FRONT = 2
STRIDE = 1024
RUN = 8
REACH = 3
BOTH = ("rep", "blk")


def routed(value, target):
    n_rep, n_blk = lax.axis_size("rep"), lax.axis_size("blk")
    route = []
    for r in range(n_rep):
        for b in range(n_blk):
            r2, b2 = target(r, b)
            route.append((r * n_blk + b, r2 * n_blk + b2 % n_blk))
    return lax.ppermute(value, BOTH, route)


def upward(value):
    return routed(value, lambda r, b: (1 - r if (b // 2) % RUN == RUN - 1 else r, b + 2))


def downward(value):
    return routed(value, lambda r, b: (1 - r if (b // 2) % RUN == 0 else r, b - 2))


def other_replica(value):
    return routed(value, lambda r, b: (1 - r, b))


def other_core(value):
    return routed(value, lambda r, b: (r, b ^ 1))


def split(x):
    high = x.astype(jnp.bfloat16)
    low = (x - high.astype(jnp.float32)).astype(jnp.bfloat16)
    return high, low


def product(a, b):
    a_high, a_low = split(a)
    b_high, b_low = split(b)

    def dot(x, y):
        return jnp.dot(x, y, preferred_element_type=jnp.float32)

    return dot(a_high, b_high) + (dot(a_high, b_low) + dot(a_low, b_high))


def scan_kernel(n_early, info, a_rows, a_cols, c_rows, c_cols, *refs):
    notes, (told, *lists) = refs[:-5], refs[-5:]
    for i in range(told.shape[0]):
        told[i] = 0
    for p in range(len(notes)):
        group = info[p]
        late = int(p >= n_early)
        work, hits = lists[2 * late], lists[2 * late + 1]

        @pl.when(group >= 0)
        def _():
            @pl.loop(0, notes[p][2 * PANEL])
            def _(q):
                @pl.loop(0, A_SLOTS)
                def _(m):
                    slot = group * A_SLOTS + m

                    @pl.when(a_cols[slot] == notes[p][q])
                    def _():
                        row, col = a_rows[slot], notes[p][PANEL + q]
                        mask, head = jnp.int32(0), jnp.int32(0)
                        for t in range(c_rows.shape[0]):
                            hit = (c_rows[t] == row) & (c_cols[t] == col)
                            mask = mask + jnp.where(hit, 1 << t, 0)
                            head = jnp.where(hit, t, head)

                        @pl.when(mask != 0)
                        def _():
                            n = told[1 + late]
                            place = ((p - late * n_early) * A_SLOTS + m) * PANEL + q
                            work[n] = head * STRIDE + place
                            hits[n] = mask
                            told[1 + late] = n + 1
                            told[0] = told[0] | mask


def scan(info, tables, notes, n_early):
    smem = pl.BlockSpec(memory_space=pltpu.SMEM)
    sizes = [8] + 2 * [n_early * A_SLOTS * PANEL] + 2 * [(len(notes) - n_early) * A_SLOTS * PANEL]
    return pl.pallas_call(
        functools.partial(scan_kernel, n_early),
        out_shape=[jax.ShapeDtypeStruct((n,), jnp.int32) for n in sizes],
        in_specs=[smem] * (5 + len(notes)),
        out_specs=[smem] * 5,
        compiler_params=pltpu.CompilerParams(vmem_limit_bytes=2**20),
        name="scan",
    )(info, *tables, *notes)


def multiply_kernel(n_whole, n_split, last, info, told, work, hits, *refs):
    n_known = info.shape[0] // 2
    base = n_known - n_split if last else 0
    if last:
        theirs, c_rows, c_cols, refs = *refs[:3], refs[3:]
    a_hbm, refs = refs[0], refs[1:]
    whole, refs = refs[:n_whole], refs[n_whole:]
    pieces, refs = refs[: 4 * n_split], refs[4 * n_split :]
    if last:
        acc_in, keep_out, send_out, plan, refs = *refs[:4], refs[4:]
    else:
        acc_out, refs = refs[0], refs[1:]
    acc, a_buf, b_buf, sems, acc_sem = refs
    size = a_buf.shape[-1]
    n_targets = acc.shape[0]
    half = n_targets // 2

    if last:
        load = pltpu.make_async_copy(acc_in, acc, acc_sem.at[0])
        load.start()

    per_panel = A_SLOTS * PANEL
    total = told[1 + int(last)]

    def fetch_b(source, buf):
        pltpu.make_async_copy(source, b_buf.at[buf], sems.at[1, buf]).start()

    def fetch(n, buf):
        i = lax.rem(work[n], STRIDE)
        panel = lax.div(i, per_panel)
        rest = lax.rem(i, per_panel)
        a_slot = info[base + panel] * A_SLOTS + lax.div(rest, PANEL)
        q = lax.rem(rest, PANEL)
        pltpu.make_async_copy(a_hbm.at[a_slot], a_buf.at[buf], sems.at[0, buf]).start()
        for p in range(n_whole):

            @pl.when(panel == p)
            def _():
                fetch_b(whole[p].at[q], buf)

        second = (lax.rem(q, 2) != info[n_known + base + panel]).astype(jnp.int32)
        place = lax.div(q, 2)
        tail = (place == FRONT).astype(jnp.int32)
        which = (panel - n_whole) * 4 + tail * 2 + second
        row = pl.multiple_of((place - tail * FRONT) * size, size)
        for p in range(4 * n_split):

            @pl.when(which == p)
            def _():
                if p % 4 < 2:
                    fetch_b(pieces[p].at[pl.ds(row, size), :], buf)
                else:
                    fetch_b(pieces[p].at[pl.ds((p % 4 - 2) * size if pieces[p].shape[0] > size else 0, size), :], buf)

    @pl.when(total > 0)
    def _():
        fetch(0, 0)

    if last:
        load.wait()
    else:
        acc[...] = jnp.zeros_like(acc)

    @pl.loop(0, total)
    def _(n):
        buf = lax.rem(n, 2)

        @pl.when(n + 1 < total)
        def _():
            fetch(n + 1, 1 - buf)

        pltpu.make_async_copy(a_hbm.at[0], a_buf.at[buf], sems.at[0, buf]).wait()
        pltpu.make_async_copy(a_hbm.at[0], b_buf.at[buf], sems.at[1, buf]).wait()
        term = product(a_buf[buf], b_buf[buf])
        head = lax.div(work[n], STRIDE)
        acc[head] = acc[head] + term

        @pl.when(hits[n] != lax.shift_left(jnp.int32(1), head))
        def _():
            @pl.loop(0, n_targets)
            def _(t):
                @pl.when((t != head) & (lax.rem(lax.shift_right_logical(hits[n], t), 2) == 1))
                def _():
                    acc[t] = acc[t] + term

    if last:
        kept = pltpu.make_async_copy(acc.at[pl.ds(0, half)], keep_out, acc_sem.at[1])
        kept.start()
        sent, come = jnp.int32(0), jnp.int32(0)
        for t in range(half):
            goes = lax.rem(lax.shift_right_logical(told[0], half + t), 2)
            comes = lax.rem(lax.shift_right_logical(theirs[0], half + t), 2)

            @pl.when(goes == 1)
            def _():
                pltpu.make_async_copy(acc.at[half + t], send_out.at[sent], acc_sem.at[0]).start()

            plan[8 + t] = come
            plan[16 + t] = comes
            plan[24 + t] = (c_rows[t] == c_cols[t]).astype(jnp.int32)
            sent, come = sent + goes, come + comes
        plan[0] = jnp.maximum(jnp.maximum(sent, come), 1) - 1
        for t in range(1, 8):
            plan[t] = 0

        @pl.loop(0, sent)
        def _(n):
            pltpu.make_async_copy(acc.at[half], send_out.at[n], acc_sem.at[0]).wait()

        kept.wait()
    else:
        out = pltpu.make_async_copy(acc, acc_out, acc_sem.at[0])
        out.start()
        out.wait()


def multiply(info, found, theirs, a_blocks, whole, pieces, acc, n_targets):
    n_whole, n_split = len(whole), len(pieces) // 4
    size = a_blocks.shape[-1]
    last = acc is not None
    smem = pl.BlockSpec(memory_space=pltpu.SMEM)
    anywhere = pl.BlockSpec(memory_space=pl.ANY)
    full = jax.ShapeDtypeStruct((n_targets, size, size), jnp.float32)
    part = jax.ShapeDtypeStruct((n_targets // 2, size, size), jnp.float32)
    plan = jax.ShapeDtypeStruct((32,), jnp.int32)
    numbers = [info, *found, *theirs]
    blocks = [a_blocks, *whole, *pieces] + ([acc] if last else [])

    def kernel(*refs):
        multiply_kernel(n_whole, n_split, last, *refs)

    return pl.pallas_call(
        kernel,
        out_shape=[part, part, plan] if last else full,
        in_specs=[smem] * len(numbers) + [anywhere] * len(blocks),
        out_specs=[anywhere, anywhere, smem] if last else anywhere,
        scratch_shapes=[
            pltpu.VMEM((n_targets, size, size), jnp.float32),
            pltpu.VMEM((2, size, size), jnp.float32),
            pltpu.VMEM((2, size, size), jnp.float32),
            pltpu.SemaphoreType.DMA((2, 2)),
            pltpu.SemaphoreType.DMA((2,)),
        ],
        cost_estimate=pl.CostEstimate(
            flops=2 * 8 * size**3, bytes_accessed=12 * 2**20, transcendentals=0
        ),
        compiler_params=pltpu.CompilerParams(vmem_limit_bytes=8 * 2**20),
        name="multiply",
    )(*numbers, *blocks)


def local(a_blocks, a_rows, a_cols, b_blocks, b_rows, b_cols, b_count, c_rows, c_cols):
    replica = lax.axis_index("rep")
    index = lax.axis_index("blk")
    core = index % 2
    z = (index // 2) % RUN
    lower = replica == 0
    a_blocks = a_blocks[0]
    b_blocks = b_blocks[0]
    size = a_blocks.shape[-1]
    n_targets = c_rows.shape[1]
    half = n_targets // 2

    numbers = jnp.concatenate([b_rows[0], b_cols[0], b_count, jnp.zeros((3,), jnp.int32)])
    notes = jnp.pad(numbers.astype(jnp.float32)[None], ((0, 7), (0, size - numbers.shape[0])))
    mine = lax.dynamic_index_in_dim(
        b_blocks.reshape(HALF, 2, size, size), replica, 1, keepdims=False
    )
    front = jnp.concatenate([mine[:FRONT].reshape(FRONT * size, size), notes], 0)
    up = down = front
    up_tail = down_tail = mine[FRONT]

    def own_first(x):
        return jnp.where(lower, x, jnp.roll(x, half))

    target_rows = own_first(c_rows[0])
    target_cols = own_first(c_cols[0])
    tables = [a_rows[0], a_cols[0], target_rows, target_cols]

    def group_of(distance):
        group = distance + jnp.where(lower, STEPS, 0)
        return jnp.where((group >= 0) & (group < STEPS), group, -1)

    def noted(piece):
        return piece[FRONT * size, : numbers.shape[0]].astype(jnp.int32)

    side = jnp.where(lower, -1, 1)
    zero = jnp.int32(0)

    ups, downs, up_tails, down_tails = [], [], [], []
    for _ in range(1, REACH + 1):
        up, down = upward(up), downward(down)
        up_tail, down_tail = upward(up_tail), downward(down_tail)
        ups.append(up)
        downs.append(down)
        up_tails.append(up_tail)
        down_tails.append(down_tail)
    partner = other_core(b_blocks)
    notes = [numbers, other_core(numbers)]
    stages = [([], notes, [group_of(zero), group_of(1 - 2 * core)], [zero, zero])]
    for s in range(1, REACH + 1):
        up, down, up_tail, down_tail = ups[s - 1], downs[s - 1], up_tails[s - 1], down_tails[s - 1]
        kept, given = jnp.where(lower, up, down), jnp.where(lower, down, up)
        rest = other_replica(given)
        kept_tail = jnp.where(lower, up_tail, down_tail)
        rest_tail = other_replica(jnp.where(lower, down_tail, up_tail))
        kept2, rest2 = other_core(kept), other_core(rest)
        tails = jnp.concatenate([kept_tail, rest_tail], 0)
        tails2 = other_core(tails)
        crossed = jnp.where(lower, z < s, z + s > RUN - 1).astype(jnp.int32)
        low = lax.bitwise_xor(replica, crossed)
        notes = [noted(kept), noted(kept2)]
        groups = [group_of(2 * s * side), group_of(2 * s * side + 1 - 2 * core)]
        pieces = [kept, rest, tails, tails, kept2, rest2, tails2, tails2]
        stages.append((pieces, notes, groups, [low, low]))

    def of(part, i):
        return [x for stage in part for x in stage[i]]

    early, late = stages[:REACH], stages[REACH:]
    info = jnp.stack(of(stages, 2) + of(stages, 3))
    told, work0, hits0, work1, hits1 = scan(
        info, tables, of(stages, 1), len(of(early, 1))
    )
    theirs = other_replica(told)
    acc = multiply(
        info, [told, work0, hits0], [], a_blocks, [b_blocks, partner], of(early, 0), None, n_targets
    )
    keep, send, plan = multiply(
        info,
        [told, work1, hits1],
        [theirs, target_rows, target_cols],
        a_blocks,
        [],
        of(late, 0),
        acc,
        n_targets,
    )
    result = lax.switch(
        plan[0], [functools.partial(finish, n + 1) for n in range(half)], keep, send, plan
    )
    return result[None]


def finish_kernel(plan, keep, come, out):
    t = pl.program_id(0)
    size = out.shape[-1]
    row = lax.broadcasted_iota(jnp.int32, (size, size), 0)
    col = lax.broadcasted_iota(jnp.int32, (size, size), 1)
    unit = jnp.where((row == col) & (plan[24 + t] == 1), 1.5, 0.0)

    @pl.when(plan[16 + t] == 1)
    def _():
        out[...] = unit - 0.5 * (keep[...] + come[...])

    @pl.when(plan[16 + t] == 0)
    def _():
        out[...] = unit - 0.5 * keep[...]


def finish(many, keep, send, plan):
    half, size = keep.shape[0], keep.shape[-1]
    come = other_replica(send[:many])
    block = (None, size, size)
    return pl.pallas_call(
        finish_kernel,
        out_shape=jax.ShapeDtypeStruct(keep.shape, jnp.float32),
        grid_spec=pltpu.PrefetchScalarGridSpec(
            num_scalar_prefetch=1,
            grid=(half,),
            in_specs=[
                pl.BlockSpec(block, lambda t, plan: (t, 0, 0)),
                pl.BlockSpec(block, lambda t, plan: (jnp.minimum(plan[8 + t], many - 1), 0, 0)),
            ],
            out_specs=pl.BlockSpec(block, lambda t, plan: (t, 0, 0)),
        ),
        compiler_params=pltpu.CompilerParams(
            dimension_semantics=("arbitrary",), vmem_limit_bytes=4 * 2**20
        ),
        name="finish",
    )(plan, keep, come)


def solution(mesh):
    return jax.shard_map(
        local,
        mesh=mesh,
        in_specs=(
            P("blk", "rep", None, None),
            P("blk", "rep"),
            P("blk", "rep"),
            P("blk", None, None, None),
            P("blk", None),
            P("blk", None),
            P("blk"),
            P("blk", None),
            P("blk", None),
        ),
        out_specs=P("blk", "rep", None, None),
        check_vma=False,
    )
```
